128 devices in a mesh: gx: 8 (over y, core), gy: 16 (over x, z).
Axes of the slice: x: 4, y: 4, z: 4, core: 2. Of those that a mesh axis runs over, the one named last changes fastest.
Arguments:
- right_side: float32 [16384, 64, 128], P(('gx', 'gy')), may hold values from -24 to 24
- fine_coupling: bfloat16 [16384, 64, 4, 64], P(('gx', 'gy')), may hold values from -0.359375 to 0.359375
- fine_diagonal: bfloat16 [16384, 64, 64], P(('gx', 'gy')), may hold values from -0.41 to 6, as said below
- fine_inverse: bfloat16 [16384, 64, 64], P(('gx', 'gy')), may hold values from -1 to 1, as said below
- coarse_coupling: bfloat16 [8192, 64, 8, 64], P(('gx', 'gy')), may hold values from -0.23925781 to 0.23925781
- coarse_diagonal: bfloat16 [8192, 64, 64], P(('gx', 'gy')), may hold values from -0.41 to 6, as said below
- coarse_inverse: bfloat16 [8192, 64, 64], P(('gx', 'gy')), may hold values from -1 to 1, as said below
- coarse_pattern: int32 [8192, 8], P(('gx', 'gy')), may hold values from 0 to 8191, as said below
Outputs:
- fine_iterate: float32 [16384, 64, 128], P(('gx', 'gy'))
- coarse_iterate: float32 [8192, 64, 128], P(('gx', 'gy'))
- next_right_side: float32 [4096, 64, 128], P(('gx', 'gy'))
The draws below stay inside these ranges and needn't reach their ends.
Inputs may be any that keep to these rules, and one draw needn't show every extreme that they name: `coarse_pattern`: the entries of cell c name the eight cells around c on the next level's grid, each once, in an order that differs from cell to cell; an entry whose cell would lie outside the grid names c itself. `fine_diagonal`: each block is a positive diagonal plus smaller off-diagonal entries. `fine_inverse`: each block is the bfloat16 rounding of the inverse of the corresponding diagonal block before its rounding. `coarse_diagonal`: each block is a positive diagonal plus smaller off-diagonal entries. `coarse_inverse`: each block is the bfloat16 rounding of the inverse of the corresponding diagonal block before its rounding.
All inputs are finite; a program needn't handle non-finite values.
Results may differ from the reference program's by a relative error of at most 0.00065.
Values sent between devices are 32-bit elements; how exact they have to be, the bound alone decides.
A program may use at most 192 MiB of HBM per device.

```python
import math
import jax
import jax.numpy as jnp
from jax import lax

SPECIES = 64
VECTORS = 128
FINE_NEIGHBOURS = 4
COARSE_NEIGHBOURS = 8
BLOCK_X = 4
BLOCK_Y = 32
GRID_X = 32
GRID_Y = 512
FINE_CELLS = 16384
COARSE_CELLS = 8192


def block_pair(key, cell_count, level_tag):
    first_key, second_key = jax.random.split(jax.random.fold_in(key, level_tag))
    leading = jnp.exp(jax.random.uniform(first_key, (cell_count, SPECIES), minval=math.log(3.0), maxval=math.log(6.0)))
    spread_part = jnp.clip(0.12 * jax.random.normal(second_key, (cell_count, SPECIES, SPECIES)), -0.4, 0.4)
    identity = jnp.eye(SPECIES, dtype=jnp.float32)
    blocks = spread_part * (1.0 - identity) + identity * leading[:, :, None]
    inverses = jnp.linalg.inv(blocks)
    return (blocks, inverses)


def draw_fine_diagonal(key, part):
    return block_pair(key, FINE_CELLS, 21)[0].astype(jnp.bfloat16)


def draw_fine_inverse(key, part):
    return block_pair(key, FINE_CELLS, 21)[1].astype(jnp.bfloat16)


def draw_coarse_diagonal(key, part):
    return block_pair(key, COARSE_CELLS, 22)[0].astype(jnp.bfloat16)


def draw_coarse_inverse(key, part):
    return block_pair(key, COARSE_CELLS, 22)[1].astype(jnp.bfloat16)


def draw_coarse_pattern(key, part):
    rows_block = BLOCK_X // 2
    cols_block = BLOCK_Y
    grid_rows = GRID_X // 2
    grid_cols = GRID_Y
    cell_count = grid_rows * grid_cols
    numbers = jnp.arange(cell_count, dtype=jnp.int32)
    per_block = rows_block * cols_block
    blocks_across = grid_cols // cols_block
    owner_block = numbers // per_block
    inside = numbers % per_block
    row_place = owner_block // blocks_across * rows_block + inside // cols_block
    col_place = owner_block % blocks_across * cols_block + inside % cols_block
    row_steps = jnp.array([-1, -1, -1, 0, 0, 1, 1, 1], dtype=jnp.int32)
    col_steps = jnp.array([-1, 0, 1, -1, 1, -1, 0, 1], dtype=jnp.int32)
    row_near = row_place[:, None] + row_steps[None, :]
    col_near = col_place[:, None] + col_steps[None, :]
    inside_grid = (row_near >= 0) & (row_near < grid_rows) & (col_near >= 0) & (col_near < grid_cols)
    target = (row_near // rows_block * blocks_across + col_near // cols_block) * per_block
    target = target + row_near % rows_block * cols_block + col_near % cols_block
    target = jnp.where(inside_grid, target, numbers[:, None])
    scores = jax.random.randint(jax.random.fold_in(key, 12), (cell_count, 8), 0, 1 << 20, dtype=jnp.int32) * 8
    scores = scores + jnp.arange(8, dtype=jnp.int32)[None, :]
    order = jnp.argsort(scores, axis=1)
    picked = jnp.take_along_axis(target, order, axis=1)
    return picked.astype(jnp.int32)


def shard_levels(key, shape, cuts, smallest, top_value):
    factor_of = 1.0
    for dim, blocks in cuts:
        steps = jax.random.uniform(jax.random.fold_in(jax.random.fold_in(key, 6), dim), (blocks,), jnp.float32, smallest / len(cuts), top_value / len(cuts))
        factor_of = factor_of * jnp.repeat(jnp.exp(steps), shape[dim] // blocks).reshape((-1,) + (1,) * (len(shape) - 1 - dim))
    return factor_of


def centred(key, shape, width, limit, cuts=(), held_as=jnp.bfloat16):
    drawn = width * jax.random.normal(key, shape, jnp.float32)
    if cuts:
        drawn = drawn * shard_levels(key, shape, cuts, -0.22, 0.18)
    return jnp.clip(drawn, -limit, limit).astype(held_as)


def setup_inputs(seed: int = 0) -> dict:
    splits = jax.random.split(jax.random.key(seed), 9)
    right_side = centred(splits[0], (FINE_CELLS, SPECIES, VECTORS), 4.0, 24.0, ((0, 128),), jnp.float32)
    fine_coupling = centred(splits[1], (FINE_CELLS, SPECIES, FINE_NEIGHBOURS, SPECIES), 0.06, 0.359375, ((0, 128),))
    fine_diagonal = draw_fine_diagonal(jax.random.fold_in(splits[8], 71), 0)
    fine_inverse = draw_fine_inverse(jax.random.fold_in(splits[8], 71), 0)
    coarse_coupling = centred(splits[4], (COARSE_CELLS, SPECIES, COARSE_NEIGHBOURS, SPECIES), 0.04, 0.23925781, ((0, 128),))
    coarse_diagonal = draw_coarse_diagonal(jax.random.fold_in(splits[8], 71), 0)
    coarse_inverse = draw_coarse_inverse(jax.random.fold_in(splits[8], 71), 0)
    coarse_pattern = draw_coarse_pattern(jax.random.fold_in(splits[8], 71), 0)
    return {"right_side": right_side, "fine_coupling": fine_coupling, "fine_diagonal": fine_diagonal, "fine_inverse": fine_inverse, "coarse_coupling": coarse_coupling, "coarse_diagonal": coarse_diagonal, "coarse_inverse": coarse_inverse, "coarse_pattern": coarse_pattern}


def to_grid(field, rows_block, cols_block, grid_rows, grid_cols):
    species, vectors = (field.shape[1], field.shape[2])
    shaped = field.reshape(grid_rows // rows_block, grid_cols // cols_block, rows_block, cols_block, species, vectors)
    return jnp.transpose(shaped, (0, 2, 1, 3, 4, 5)).reshape(grid_rows, grid_cols, species, vectors)

def per_cell(matrix, vector_b, block_size):
    block_count = vector_b.shape[0] // block_size

    def one_block(number):
        start_cell = number * block_size
        matrix_part = lax.dynamic_slice_in_dim(matrix, start_cell, block_size, 0).astype(jnp.float32)
        vector_part = lax.dynamic_slice_in_dim(vector_b, start_cell, block_size, 0)
        return jnp.einsum('cij,cjv->civ', matrix_part, vector_part, precision=lax.Precision.HIGHEST)
    result = lax.map(one_block, jnp.arange(block_count, dtype=jnp.int32))
    return result.reshape(-1, vector_b.shape[1], vector_b.shape[2])

def operate(vector_b, near_fn, coupling, diagonal, block_size):
    block_count = vector_b.shape[0] // block_size

    def one_block(number):
        start_cell = number * block_size
        near_part = near_fn(number)
        coupling_part = lax.dynamic_slice_in_dim(coupling, start_cell, block_size, 0).astype(jnp.float32)
        diagonal_part = lax.dynamic_slice_in_dim(diagonal, start_cell, block_size, 0).astype(jnp.float32)
        own_part = lax.dynamic_slice_in_dim(vector_b, start_cell, block_size, 0)
        summed = jnp.einsum('cikj,ckjv->civ', coupling_part, near_part, precision=lax.Precision.HIGHEST)
        return summed + jnp.einsum('cij,cjv->civ', diagonal_part, own_part, precision=lax.Precision.HIGHEST)
    result = lax.map(one_block, jnp.arange(block_count, dtype=jnp.int32))
    return result.reshape(-1, vector_b.shape[1], vector_b.shape[2])

def fine_maker(vector_b):
    grid = to_grid(vector_b, BLOCK_X, BLOCK_Y, GRID_X, GRID_Y)
    padded = jnp.pad(grid, ((1, 1), (1, 1), (0, 0), (0, 0)))
    blocks_across = GRID_Y // BLOCK_Y
    species, vectors = (vector_b.shape[1], vector_b.shape[2])

    def near_fn(number):
        row_start = number // blocks_across * BLOCK_X
        col_start = number % blocks_across * BLOCK_Y
        zero = jnp.zeros((), jnp.int32)
        window = lax.dynamic_slice(padded, (row_start, col_start, zero, zero), (BLOCK_X + 2, BLOCK_Y + 2, species, vectors))
        pieces = [window[:-2, 1:-1], window[2:, 1:-1], window[1:-1, :-2], window[1:-1, 2:]]
        return jnp.stack(pieces, axis=2).reshape(BLOCK_X * BLOCK_Y, 4, species, vectors)
    return near_fn

def smooth(side, coupling, diagonal, inverse, maker, block_size):
    first_sweep = per_cell(inverse, side, block_size)
    slack_part = side - operate(first_sweep, maker(first_sweep), coupling, diagonal, block_size)
    second = first_sweep + per_cell(inverse, slack_part, block_size)
    residue = side - operate(second, maker(second), coupling, diagonal, block_size)
    return (second, residue)

def reference(right_side, fine_coupling, fine_diagonal, fine_inverse, coarse_coupling, coarse_diagonal, coarse_inverse, coarse_pattern):
    half_rows = BLOCK_X // 2
    coarse_block = half_rows * BLOCK_Y
    fine_iterate, fine_residue = smooth(right_side, fine_coupling, fine_diagonal, fine_inverse, fine_maker, BLOCK_X * BLOCK_Y)
    coarse_side = fine_residue.reshape(-1, half_rows, 2, BLOCK_Y, SPECIES, VECTORS).sum(axis=2).reshape(-1, SPECIES, VECTORS)
    columns = coarse_pattern.astype(jnp.int32)

    def coarse_maker(vector_b):

        def near_fn(number):
            rows = lax.dynamic_slice_in_dim(columns, number * coarse_block, coarse_block, 0)
            return jnp.take(vector_b, rows, axis=0)
        return near_fn
    coarse_iterate, coarse_residue = smooth(coarse_side, coarse_coupling, coarse_diagonal, coarse_inverse, coarse_maker, coarse_block)
    next_side = coarse_residue.reshape(-1, half_rows, BLOCK_Y // 2, 2, SPECIES, VECTORS).sum(axis=3).reshape(-1, SPECIES, VECTORS)
    return (fine_iterate, coarse_iterate, next_side)
```

```python
import functools

import jax
import jax.numpy as jnp
from jax import lax
from jax.experimental import pallas as pl
from jax.experimental.pallas import tpu as pltpu
from jax.sharding import PartitionSpec as P

BLOCK_X = 4
BLOCK_Y = 32
HALF_X = BLOCK_X // 2
S = 64
V = 128
CW = 8
STEPS = BLOCK_Y // CW
VMEM_LIMIT = 60 * 1024 * 1024


def window_index(pattern, rows_block, cols_block, anchor_rows, anchor_cols):
    per_block = rows_block * cols_block
    blocks_across = lax.axis_size("gy")
    owner_block = pattern // per_block
    inside = pattern % per_block
    row_place = owner_block // blocks_across * rows_block + inside // cols_block
    col_place = owner_block % blocks_across * cols_block + inside % cols_block
    index = (row_place - anchor_rows + 1) * (cols_block + 2) + (col_place - anchor_cols + 1)
    return jnp.clip(index, 0, (rows_block + 2) * (cols_block + 2) - 1)


def split(x):
    high = x.astype(jnp.bfloat16)
    low = (x - high.astype(jnp.float32)).astype(jnp.bfloat16)
    return jnp.concatenate([high, low], axis=-1)


def dot(matrix, halves):
    return jnp.dot(matrix, halves, preferred_element_type=jnp.float32)


def merge(x):
    return x[:, :V] + x[:, V:]


def first_kernel(b_ref, inv_ref, out_ref):
    def cell(i, carry):
        out_ref[i] = merge(dot(inv_ref[i], split(b_ref[i])))
        return carry

    lax.fori_loop(0, b_ref.shape[0], cell, 0, unroll=4)


def first_sweep(b, inverse):
    cells = b.shape[0]
    block = 16
    return pl.pallas_call(
        first_kernel,
        grid=(cells // block,),
        in_specs=[
            pl.BlockSpec((block, S, V), lambda i: (i, 0, 0)),
            pl.BlockSpec((block, S, S), lambda i: (i, 0, 0)),
        ],
        out_specs=pl.BlockSpec((block, S, V), lambda i: (i, 0, 0)),
        out_shape=jax.ShapeDtypeStruct((cells, S, V), jnp.float32),
        compiler_params=pltpu.CompilerParams(vmem_limit_bytes=VMEM_LIMIT),
        cost_estimate=pl.CostEstimate(
            flops=cells * S * S * V * 4, bytes_accessed=cells * S * (V * 8 + S * 2), transcendentals=0
        ),
        name="first",
    )(b, inverse)


def fill_fine(window, x_ref, up_ref, down_ref, left_ref, right_ref):
    @pl.when((pl.program_id(0) == 0) & (pl.program_id(1) == 0))
    def _():
        def column(y, carry):
            for x in range(BLOCK_X):
                window[x + 1, y + 1] = split(x_ref[x, y])
            window[0, y + 1] = split(up_ref[0, y])
            window[BLOCK_X + 1, y + 1] = split(down_ref[0, y])
            return carry

        lax.fori_loop(0, BLOCK_Y, column, 0)
        for x in range(BLOCK_X):
            window[x + 1, 0] = split(left_ref[x, 0])
            window[x + 1, BLOCK_Y + 1] = split(right_ref[x, 0])


def fine_remainder(window, coup_ref, diag_ref, b_ref, x, y, row, col):
    near = jnp.concatenate(
        [
            window[row, col + 1],
            window[row + 2, col + 1],
            window[row + 1, col],
            window[row + 1, col + 2],
        ],
        axis=0,
    )
    total = dot(coup_ref[x, y], near) + dot(diag_ref[x, y], window[row + 1, col + 1])
    return b_ref[x, y] - merge(total)


def fine_smooth_kernel(
    x_ref, up_ref, down_ref, left_ref, right_ref, coup_ref, diag_ref, inv_ref, b_ref, out_ref, window
):
    fill_fine(window, x_ref, up_ref, down_ref, left_ref, right_ref)
    row0 = pl.program_id(0) * 2
    col0 = pl.program_id(1) * CW

    def column(y, carry):
        for x in range(2):
            slack = fine_remainder(window, coup_ref, diag_ref, b_ref, x, y, row0 + x, col0 + y)
            out_ref[x, y] = x_ref[row0 + x, col0 + y] + merge(dot(inv_ref[x, y], split(slack)))
        return carry

    lax.fori_loop(0, CW, column, 0, unroll=2)


def fine_residue_kernel(
    x_ref, up_ref, down_ref, left_ref, right_ref, coup_ref, diag_ref, b_ref, inv_ref, side_ref, out_ref, window
):
    fill_fine(window, x_ref, up_ref, down_ref, left_ref, right_ref)
    row0 = pl.program_id(0) * 2
    col0 = pl.program_id(1) * CW

    def column(y, carry):
        side = fine_remainder(window, coup_ref, diag_ref, b_ref, 0, y, row0, col0 + y)
        side = side + fine_remainder(window, coup_ref, diag_ref, b_ref, 1, y, row0 + 1, col0 + y)
        side_ref[0, y] = side
        out_ref[0, y] = merge(dot(inv_ref[0, y], split(side)))
        return carry

    lax.fori_loop(0, CW, column, 0, unroll=2)


def whole(shape):
    return pl.BlockSpec(shape, lambda r, j: (0,) * len(shape))


def part(rows, cols, *rest):
    return pl.BlockSpec((rows, cols) + rest, lambda r, j: (r, j) + (0,) * len(rest))


FINE_FIELD = [
    whole((BLOCK_X, BLOCK_Y, S, V)),
    whole((1, BLOCK_Y, S, V)),
    whole((1, BLOCK_Y, S, V)),
    whole((BLOCK_X, 1, S, V)),
    whole((BLOCK_X, 1, S, V)),
]


def fine_cost(steps):
    cells = BLOCK_X * BLOCK_Y
    return pl.CostEstimate(
        flops=cells * steps * S * S * V * 4, bytes_accessed=cells * S * (V * 12 + 768), transcendentals=0
    )


def fine_smooth(field, coupling, diagonal, inverse, b):
    return pl.pallas_call(
        fine_smooth_kernel,
        grid=(HALF_X, STEPS),
        in_specs=FINE_FIELD
        + [part(2, CW, S, 4 * S), part(2, CW, S, S), part(2, CW, S, S), part(2, CW, S, V)],
        out_specs=part(2, CW, S, V),
        out_shape=jax.ShapeDtypeStruct((BLOCK_X, BLOCK_Y, S, V), jnp.float32),
        scratch_shapes=[pltpu.VMEM((BLOCK_X + 2, BLOCK_Y + 2, S, 2 * V), jnp.bfloat16)],
        compiler_params=pltpu.CompilerParams(vmem_limit_bytes=VMEM_LIMIT),
        cost_estimate=fine_cost(6),
        name="fine_smooth",
    )(*field, coupling, diagonal, inverse, b)


def fine_residue(field, coupling, diagonal, b, coarse_inverse):
    shape = jax.ShapeDtypeStruct((HALF_X, BLOCK_Y, S, V), jnp.float32)
    return pl.pallas_call(
        fine_residue_kernel,
        grid=(HALF_X, STEPS),
        in_specs=FINE_FIELD
        + [part(2, CW, S, 4 * S), part(2, CW, S, S), part(2, CW, S, V), part(1, CW, S, S)],
        out_specs=[part(1, CW, S, V), part(1, CW, S, V)],
        out_shape=[shape, shape],
        scratch_shapes=[pltpu.VMEM((BLOCK_X + 2, BLOCK_Y + 2, S, 2 * V), jnp.bfloat16)],
        compiler_params=pltpu.CompilerParams(vmem_limit_bytes=VMEM_LIMIT),
        cost_estimate=fine_cost(6),
        name="fine_residue",
    )(*field, coupling, diagonal, b, coarse_inverse)


WIDTH = BLOCK_Y + 2


def fill_coarse(window, x_ref, up_ref, down_ref, left_ref, right_ref, corner_ref):
    @pl.when((pl.program_id(0) == 0) & (pl.program_id(1) == 0))
    def _():
        def column(y, carry):
            for x in range(HALF_X):
                window[(x + 1) * WIDTH + y + 1] = split(x_ref[x, y])
            window[y + 1] = split(up_ref[0, y])
            window[(HALF_X + 1) * WIDTH + y + 1] = split(down_ref[0, y])
            return carry

        lax.fori_loop(0, BLOCK_Y, column, 0)
        for x in range(HALF_X):
            window[(x + 1) * WIDTH] = split(left_ref[x, 0])
            window[(x + 1) * WIDTH + BLOCK_Y + 1] = split(right_ref[x, 0])
        window[0] = split(corner_ref[0])
        window[BLOCK_Y + 1] = split(corner_ref[1])
        window[(HALF_X + 1) * WIDTH] = split(corner_ref[2])
        window[(HALF_X + 1) * WIDTH + BLOCK_Y + 1] = split(corner_ref[3])


def coarse_remainder(index_ref, window, coup_ref, diag_ref, b_ref, y, row, col):
    place = (row * BLOCK_Y + col) * 8
    near = [window[index_ref[place + k]] for k in range(8)]
    matrix = coup_ref[0, y]
    total = dot(matrix[:, : 4 * S], jnp.concatenate(near[:4], axis=0))
    total = total + dot(matrix[:, 4 * S :], jnp.concatenate(near[4:], axis=0))
    total = total + dot(diag_ref[0, y], window[(row + 1) * WIDTH + col + 1])
    return b_ref[0, y] - merge(total)


def coarse_smooth_kernel(
    index_ref, x_ref, up_ref, down_ref, left_ref, right_ref, corner_ref,
    coup_ref, diag_ref, inv_ref, b_ref, out_ref, window,
):
    fill_coarse(window, x_ref, up_ref, down_ref, left_ref, right_ref, corner_ref)
    row = pl.program_id(0)
    col0 = pl.program_id(1) * CW

    def column(y, carry):
        slack = coarse_remainder(index_ref, window, coup_ref, diag_ref, b_ref, y, row, col0 + y)
        out_ref[0, y] = x_ref[row, col0 + y] + merge(dot(inv_ref[0, y], split(slack)))
        return carry

    lax.fori_loop(0, CW, column, 0, unroll=2)


def coarse_residue_kernel(
    index_ref, x_ref, up_ref, down_ref, left_ref, right_ref, corner_ref,
    coup_ref, diag_ref, b_ref, out_ref, window,
):
    fill_coarse(window, x_ref, up_ref, down_ref, left_ref, right_ref, corner_ref)
    row = pl.program_id(0)
    col0 = pl.program_id(1) * CW

    def column(y, carry):
        low = coarse_remainder(index_ref, window, coup_ref, diag_ref, b_ref, 2 * y, row, col0 + 2 * y)
        high = coarse_remainder(index_ref, window, coup_ref, diag_ref, b_ref, 2 * y + 1, row, col0 + 2 * y + 1)
        out_ref[0, y] = low + high
        return carry

    lax.fori_loop(0, CW // 2, column, 0)


def whole_c(shape):
    return pl.BlockSpec(shape, lambda r, j, index: (0,) * len(shape))


def part_c(rows, cols, *rest):
    return pl.BlockSpec((rows, cols) + rest, lambda r, j, index: (r, j) + (0,) * len(rest))


COARSE_FIELD = [
    whole_c((HALF_X, BLOCK_Y, S, V)),
    whole_c((1, BLOCK_Y, S, V)),
    whole_c((1, BLOCK_Y, S, V)),
    whole_c((HALF_X, 1, S, V)),
    whole_c((HALF_X, 1, S, V)),
    whole_c((4, S, V)),
]


def coarse_call(kernel, name, index, field, matrices, matrix_specs, out_cols):
    cells = HALF_X * BLOCK_Y
    return pl.pallas_call(
        kernel,
        grid_spec=pltpu.PrefetchScalarGridSpec(
            num_scalar_prefetch=1,
            grid=(HALF_X, STEPS),
            in_specs=COARSE_FIELD + matrix_specs,
            out_specs=part_c(1, out_cols // STEPS, S, V),
            scratch_shapes=[pltpu.VMEM(((HALF_X + 2) * WIDTH, S, 2 * V), jnp.bfloat16)],
        ),
        out_shape=jax.ShapeDtypeStruct((HALF_X, out_cols, S, V), jnp.float32),
        compiler_params=pltpu.CompilerParams(vmem_limit_bytes=VMEM_LIMIT),
        cost_estimate=pl.CostEstimate(
            flops=cells * 10 * S * S * V * 4, bytes_accessed=cells * S * (V * 12 + 1280), transcendentals=0
        ),
        name=name,
    )(index, *field, *matrices)


def steps_of(axis):
    forward = [(i, i + 1) for i in range(lax.axis_size(axis) - 1)]
    return forward, [(target, source) for source, target in forward]


def edges(grid):
    down, up = steps_of("gx")
    right, left = steps_of("gy")
    return [
        lax.ppermute(grid[-1:], "gx", down),
        lax.ppermute(grid[:1], "gx", up),
        lax.ppermute(grid[:, -1:], "gy", right),
        lax.ppermute(grid[:, :1], "gy", left),
    ]


def corners(grid):
    rows, cols = lax.axis_size("gx"), lax.axis_size("gy")
    taken = []
    for row_step, col_step in ((-1, -1), (-1, 1), (1, -1), (1, 1)):
        pairs = []
        for r in range(rows):
            for c in range(cols):
                if 0 <= r + row_step < rows and 0 <= c + col_step < cols:
                    pairs.append(((r + row_step) * cols + c + col_step, r * cols + c))
        x = -1 if row_step < 0 else 0
        y = -1 if col_step < 0 else 0
        taken.append(lax.ppermute(grid[x, y][None], ("gx", "gy"), pairs))
    return jnp.concatenate(taken, axis=0)


def on_device(
    right_side,
    fine_coupling,
    fine_diagonal,
    fine_inverse,
    coarse_coupling,
    coarse_diagonal,
    coarse_inverse,
    coarse_pattern,
):
    index = window_index(
        coarse_pattern,
        HALF_X,
        BLOCK_Y,
        lax.axis_index("gx") * HALF_X,
        lax.axis_index("gy") * BLOCK_Y,
    ).reshape(-1)

    def fine(array):
        return array.reshape((BLOCK_X, BLOCK_Y) + array.shape[1:])

    def coarse(array):
        return array.reshape((HALF_X, BLOCK_Y) + array.shape[1:])

    fine_first = fine(first_sweep(right_side, fine_inverse))
    fine_matrix = fine(fine_coupling.reshape(-1, S, 4 * S))
    coarse_matrix = coarse(coarse_coupling.reshape(-1, S, 8 * S))
    b = fine(right_side)
    fine_iterate = fine_smooth(
        [fine_first] + edges(fine_first), fine_matrix, fine(fine_diagonal), fine(fine_inverse), b
    )
    side, coarse_first = fine_residue(
        [fine_iterate] + edges(fine_iterate), fine_matrix, fine(fine_diagonal), b, coarse(coarse_inverse)
    )
    specs = [part_c(1, CW, S, 8 * S), part_c(1, CW, S, S)]
    coarse_iterate = coarse_call(
        coarse_smooth_kernel, "coarse_smooth", index,
        [coarse_first] + edges(coarse_first) + [corners(coarse_first)],
        [coarse_matrix, coarse(coarse_diagonal), coarse(coarse_inverse), side],
        specs + [part_c(1, CW, S, S), part_c(1, CW, S, V)],
        BLOCK_Y,
    )
    next_side = coarse_call(
        coarse_residue_kernel, "coarse_residue", index,
        [coarse_iterate] + edges(coarse_iterate) + [corners(coarse_iterate)],
        [coarse_matrix, coarse(coarse_diagonal), side],
        specs + [part_c(1, CW, S, V)],
        BLOCK_Y // 2,
    )
    return (
        fine_iterate.reshape(-1, S, V),
        coarse_iterate.reshape(-1, S, V),
        next_side.reshape(-1, S, V),
    )


def solution(mesh):
    cell = P(("gx", "gy"), None, None)
    placed = (
        cell,
        P(("gx", "gy"), None, None, None),
        cell,
        cell,
        P(("gx", "gy"), None, None, None),
        cell,
        cell,
        P(("gx", "gy"), None),
    )
    return jax.shard_map(
        on_device,
        mesh=mesh,
        in_specs=placed,
        out_specs=(cell, cell, cell),
        check_vma=False,
    )
```

```python
import functools

import jax
import jax.numpy as jnp
from jax import lax
from jax.experimental import pallas as pl
from jax.experimental.pallas import tpu as pltpu
from jax.sharding import PartitionSpec as P

BLOCK_X = 4
BLOCK_Y = 32
HALF_X = BLOCK_X // 2
S = 64
V = 128
CW = 8
STEPS = BLOCK_Y // CW
VMEM_LIMIT = 60 * 1024 * 1024


def window_index(pattern, rows_block, cols_block, anchor_rows, anchor_cols):
    per_block = rows_block * cols_block
    blocks_across = lax.axis_size("gy")
    owner_block = pattern // per_block
    inside = pattern % per_block
    row_place = owner_block // blocks_across * rows_block + inside // cols_block
    col_place = owner_block % blocks_across * cols_block + inside % cols_block
    index = (row_place - anchor_rows + 1) * (cols_block + 2) + (col_place - anchor_cols + 1)
    return jnp.clip(index, 0, (rows_block + 2) * (cols_block + 2) - 1)


def split(x):
    high = x.astype(jnp.bfloat16)
    low = (x - high.astype(jnp.float32)).astype(jnp.bfloat16)
    return jnp.concatenate([high, low], axis=-1)


def dot(matrix, halves):
    return jnp.dot(matrix, halves, preferred_element_type=jnp.float32)


def merge(x):
    return x[:, :V] + x[:, V:]


def first_kernel(b_ref, inv_ref, out_ref):
    def cell(step, carry):
        cells = [4 * step + i for i in range(4)]
        halves = [split(b_ref[i]) for i in cells]
        products = [merge(dot(inv_ref[i], value)) for i, value in zip(cells, halves)]
        for i, value in zip(cells, products):
            out_ref[i] = value
        return carry

    lax.fori_loop(0, b_ref.shape[0] // 4, cell, 0, unroll=2)


def first_sweep(b, inverse):
    cells = b.shape[0]
    block = 16
    return pl.pallas_call(
        first_kernel,
        grid=(cells // block,),
        in_specs=[
            pl.BlockSpec((block, S, V), lambda i: (i, 0, 0)),
            pl.BlockSpec((block, S, S), lambda i: (i, 0, 0)),
        ],
        out_specs=pl.BlockSpec((block, S, V), lambda i: (i, 0, 0)),
        out_shape=jax.ShapeDtypeStruct((cells, S, V), jnp.float32),
        compiler_params=pltpu.CompilerParams(vmem_limit_bytes=VMEM_LIMIT),
        cost_estimate=pl.CostEstimate(
            flops=cells * S * S * V * 4, bytes_accessed=cells * S * (V * 8 + S * 2), transcendentals=0
        ),
        name="first",
    )(b, inverse)


def fill_fine(window, x_ref, up_ref, down_ref, left_ref, right_ref):
    row, rows = lax.axis_index("gx"), lax.axis_size("gx")
    col, cols = lax.axis_index("gy"), lax.axis_size("gy")

    def inside(flag, value):
        return split(jnp.where(flag, value, jnp.zeros_like(value)))

    @pl.when((pl.program_id(0) == 0) & (pl.program_id(1) == 0))
    def _():
        def column(y, carry):
            for x in range(BLOCK_X):
                window[x + 1, y + 1] = split(x_ref[x, y])
            window[0, y + 1] = inside(row > 0, up_ref[0, y])
            window[BLOCK_X + 1, y + 1] = inside(row < rows - 1, down_ref[0, y])
            return carry

        lax.fori_loop(0, BLOCK_Y, column, 0)
        for x in range(BLOCK_X):
            window[x + 1, 0] = inside(col > 0, left_ref[x, 0])
            window[x + 1, BLOCK_Y + 1] = inside(col < cols - 1, right_ref[x, 0])


def fine_remainder(window, coup_ref, diag_ref, b_ref, x, y, row, col):
    near = jnp.concatenate(
        [
            window[row, col + 1],
            window[row + 2, col + 1],
            window[row + 1, col],
            window[row + 1, col + 2],
        ],
        axis=0,
    )
    total = dot(coup_ref[x, y], near) + dot(diag_ref[x, y], window[row + 1, col + 1])
    return b_ref[x, y] - merge(total)


def fine_smooth_kernel(
    x_ref, up_ref, down_ref, left_ref, right_ref, coup_ref, diag_ref, inv_ref, b_ref, out_ref, window
):
    fill_fine(window, x_ref, up_ref, down_ref, left_ref, right_ref)
    row0 = pl.program_id(0) * 2
    col0 = pl.program_id(1) * CW

    def column(step, carry):
        cells = [(x, 2 * step + y) for y in range(2) for x in range(2)]
        slack = [
            split(fine_remainder(window, coup_ref, diag_ref, b_ref, x, y, row0 + x, col0 + y))
            for x, y in cells
        ]
        for (x, y), value in zip(cells, slack):
            out_ref[x, y] = x_ref[row0 + x, col0 + y] + merge(dot(inv_ref[x, y], value))
        return carry

    lax.fori_loop(0, CW // 2, column, 0, unroll=2)


def fine_residue_kernel(
    x_ref, up_ref, down_ref, left_ref, right_ref, coup_ref, diag_ref, b_ref, inv_ref, side_ref, out_ref, window
):
    fill_fine(window, x_ref, up_ref, down_ref, left_ref, right_ref)
    row0 = pl.program_id(0) * 2
    col0 = pl.program_id(1) * CW

    def column(step, carry):
        columns = [2 * step + y for y in range(2)]
        pairs = [
            [
                fine_remainder(window, coup_ref, diag_ref, b_ref, x, y, row0 + x, col0 + y)
                for x in range(2)
            ]
            for y in columns
        ]
        sides = [low + high for low, high in pairs]
        for y, side in zip(columns, sides):
            side_ref[0, y] = side
        halves = [split(side) for side in sides]
        for y, value in zip(columns, halves):
            out_ref[0, y] = merge(dot(inv_ref[0, y], value))
        return carry

    lax.fori_loop(0, CW // 2, column, 0, unroll=2)


def whole(shape):
    return pl.BlockSpec(shape, lambda r, j: (0,) * len(shape))


def part(rows, cols, *rest):
    return pl.BlockSpec((rows, cols) + rest, lambda r, j: (r, j) + (0,) * len(rest))


FINE_FIELD = [
    whole((BLOCK_X, BLOCK_Y, S, V)),
    whole((1, BLOCK_Y, S, V)),
    whole((1, BLOCK_Y, S, V)),
    whole((BLOCK_X, 1, S, V)),
    whole((BLOCK_X, 1, S, V)),
]


def fine_cost(steps):
    cells = BLOCK_X * BLOCK_Y
    return pl.CostEstimate(
        flops=cells * steps * S * S * V * 4, bytes_accessed=cells * S * (V * 12 + 768), transcendentals=0
    )


def fine_smooth(field, coupling, diagonal, inverse, b):
    return pl.pallas_call(
        fine_smooth_kernel,
        grid=(HALF_X, STEPS),
        in_specs=FINE_FIELD
        + [part(2, CW, S, 4 * S), part(2, CW, S, S), part(2, CW, S, S), part(2, CW, S, V)],
        out_specs=part(2, CW, S, V),
        out_shape=jax.ShapeDtypeStruct((BLOCK_X, BLOCK_Y, S, V), jnp.float32),
        scratch_shapes=[pltpu.VMEM((BLOCK_X + 2, BLOCK_Y + 2, S, 2 * V), jnp.bfloat16)],
        compiler_params=pltpu.CompilerParams(vmem_limit_bytes=VMEM_LIMIT),
        cost_estimate=fine_cost(6),
        name="fine_smooth",
    )(*field, coupling, diagonal, inverse, b)


def fine_residue(field, coupling, diagonal, b, coarse_inverse):
    shape = jax.ShapeDtypeStruct((HALF_X, BLOCK_Y, S, V), jnp.float32)
    return pl.pallas_call(
        fine_residue_kernel,
        grid=(HALF_X, STEPS),
        in_specs=FINE_FIELD
        + [part(2, CW, S, 4 * S), part(2, CW, S, S), part(2, CW, S, V), part(1, CW, S, S)],
        out_specs=[part(1, CW, S, V), part(1, CW, S, V)],
        out_shape=[shape, shape],
        scratch_shapes=[pltpu.VMEM((BLOCK_X + 2, BLOCK_Y + 2, S, 2 * V), jnp.bfloat16)],
        compiler_params=pltpu.CompilerParams(vmem_limit_bytes=VMEM_LIMIT),
        cost_estimate=fine_cost(6),
        name="fine_residue",
    )(*field, coupling, diagonal, b, coarse_inverse)


WIDTH = BLOCK_Y + 2


def fill_coarse(window, x_ref, up_ref, down_ref, left_ref, right_ref, corner_refs):
    @pl.when((pl.program_id(0) == 0) & (pl.program_id(1) == 0))
    def _():
        def column(y, carry):
            for x in range(HALF_X):
                window[(x + 1) * WIDTH + y + 1] = split(x_ref[x, y])
            window[y + 1] = split(up_ref[0, y])
            window[(HALF_X + 1) * WIDTH + y + 1] = split(down_ref[0, y])
            return carry

        lax.fori_loop(0, BLOCK_Y, column, 0)
        for x in range(HALF_X):
            window[(x + 1) * WIDTH] = split(left_ref[x, 0])
            window[(x + 1) * WIDTH + BLOCK_Y + 1] = split(right_ref[x, 0])
        window[0] = split(corner_refs[0][0, 0])
        window[BLOCK_Y + 1] = split(corner_refs[1][0, 0])
        window[(HALF_X + 1) * WIDTH] = split(corner_refs[2][0, 0])
        window[(HALF_X + 1) * WIDTH + BLOCK_Y + 1] = split(corner_refs[3][0, 0])


def coarse_remainder(index_ref, window, coup_ref, diag_ref, b_ref, y, row, col):
    place = (row * BLOCK_Y + col) * 8
    near = [window[index_ref[place + k]] for k in range(8)]
    matrix = coup_ref[0, y]
    total = dot(matrix[:, : 4 * S], jnp.concatenate(near[:4], axis=0))
    total = total + dot(matrix[:, 4 * S :], jnp.concatenate(near[4:], axis=0))
    total = total + dot(diag_ref[0, y], window[(row + 1) * WIDTH + col + 1])
    return b_ref[0, y] - merge(total)


def coarse_smooth_kernel(
    index_ref, x_ref, up_ref, down_ref, left_ref, right_ref, c0_ref, c1_ref, c2_ref, c3_ref,
    coup_ref, diag_ref, inv_ref, b_ref, out_ref, window,
):
    fill_coarse(window, x_ref, up_ref, down_ref, left_ref, right_ref, (c0_ref, c1_ref, c2_ref, c3_ref))
    row = pl.program_id(0)
    col0 = pl.program_id(1) * CW

    def column(step, carry):
        cells = [4 * step + y for y in range(4)]
        slack = [
            split(coarse_remainder(index_ref, window, coup_ref, diag_ref, b_ref, y, row, col0 + y))
            for y in cells
        ]
        for y, value in zip(cells, slack):
            out_ref[0, y] = x_ref[row, col0 + y] + merge(dot(inv_ref[0, y], value))
        return carry

    lax.fori_loop(0, CW // 4, column, 0)


def coarse_residue_kernel(
    index_ref, x_ref, up_ref, down_ref, left_ref, right_ref, c0_ref, c1_ref, c2_ref, c3_ref,
    coup_ref, diag_ref, b_ref, out_ref, window,
):
    fill_coarse(window, x_ref, up_ref, down_ref, left_ref, right_ref, (c0_ref, c1_ref, c2_ref, c3_ref))
    row = pl.program_id(0)
    col0 = pl.program_id(1) * CW

    def column(step, carry):
        cells = [4 * step + y for y in range(4)]
        left = [
            coarse_remainder(index_ref, window, coup_ref, diag_ref, b_ref, y, row, col0 + y) for y in cells
        ]
        for y in range(2):
            out_ref[0, 2 * step + y] = left[2 * y] + left[2 * y + 1]
        return carry

    lax.fori_loop(0, CW // 4, column, 0)


def whole_c(shape):
    return pl.BlockSpec(shape, lambda r, j, index: (0,) * len(shape))


def part_c(rows, cols, *rest):
    return pl.BlockSpec((rows, cols) + rest, lambda r, j, index: (r, j) + (0,) * len(rest))


COARSE_FIELD = [
    whole_c((HALF_X, BLOCK_Y, S, V)),
    whole_c((1, BLOCK_Y, S, V)),
    whole_c((1, BLOCK_Y, S, V)),
    whole_c((HALF_X, 1, S, V)),
    whole_c((HALF_X, 1, S, V)),
] + [whole_c((1, 1, S, V))] * 4


def coarse_call(kernel, name, index, field, matrices, matrix_specs, out_cols):
    cells = HALF_X * BLOCK_Y
    return pl.pallas_call(
        kernel,
        grid_spec=pltpu.PrefetchScalarGridSpec(
            num_scalar_prefetch=1,
            grid=(HALF_X, STEPS),
            in_specs=COARSE_FIELD + matrix_specs,
            out_specs=part_c(1, out_cols // STEPS, S, V),
            scratch_shapes=[pltpu.VMEM(((HALF_X + 2) * WIDTH, S, 2 * V), jnp.bfloat16)],
        ),
        out_shape=jax.ShapeDtypeStruct((HALF_X, out_cols, S, V), jnp.float32),
        compiler_params=pltpu.CompilerParams(vmem_limit_bytes=VMEM_LIMIT),
        cost_estimate=pl.CostEstimate(
            flops=cells * 10 * S * S * V * 4, bytes_accessed=cells * S * (V * 12 + 1280), transcendentals=0
        ),
        name=name,
    )(index, *field, *matrices)


def steps_of(axis):
    forward = [(i, i + 1) for i in range(lax.axis_size(axis) - 1)]
    return forward, [(target, source) for source, target in forward]


def edges(grid):
    down, up = steps_of("gx")
    right, left = steps_of("gy")
    return [
        lax.ppermute(grid[-1:], "gx", down),
        lax.ppermute(grid[:1], "gx", up),
        lax.ppermute(grid[:, -1:], "gy", right),
        lax.ppermute(grid[:, :1], "gy", left),
    ]


SIDES = ((1, 0), (-1, 0), (0, 1), (0, -1))
CORNERS = ((1, 1), (1, -1), (-1, 1), (-1, -1))


def halo_kernel(ways, x_ref, *refs):
    outs, (send_sem, recv_sem) = refs[:-2], refs[-2:]
    row, rows = lax.axis_index("gx"), lax.axis_size("gx")
    col, cols = lax.axis_index("gy"), lax.axis_size("gy")

    def exists(dx, dy):
        return (row + dx >= 0) & (row + dx < rows) & (col + dy >= 0) & (col + dy < cols)

    def at(step, size):
        return {1: pl.ds(size - 1, 1), -1: pl.ds(0, 1), 0: pl.ds(0, size)}[step]

    def copy(way):
        dx, dy = ways[way]
        return pltpu.make_async_remote_copy(
            src_ref=x_ref.at[at(dx, x_ref.shape[0]), at(dy, x_ref.shape[1])],
            dst_ref=outs[way],
            send_sem=send_sem.at[way],
            recv_sem=recv_sem.at[way],
            device_id=(row + dx, col + dy),
            device_id_type=pl.DeviceIdType.MESH,
        )

    barrier = pltpu.get_barrier_semaphore()
    for dx, dy in ways:
        @pl.when(exists(dx, dy))
        def _():
            pl.semaphore_signal(
                barrier, inc=1, device_id=(row + dx, col + dy), device_id_type=pl.DeviceIdType.MESH
            )
    peers = [jnp.where(exists(dx, dy), 1, 0) for dx, dy in ways]
    pl.semaphore_wait(barrier, sum(peers[1:], peers[0]))
    for way, (dx, dy) in enumerate(ways):
        @pl.when(exists(dx, dy))
        def _():
            copy(way).start()
    for way, (dx, dy) in enumerate(ways):
        @pl.when(exists(dx, dy))
        def _():
            copy(way).wait_send()

        @pl.when(exists(-dx, -dy))
        def _():
            copy(way).wait_recv()


def halo(grid, ways, number):
    rows, cols = grid.shape[:2]
    shapes = [
        jax.ShapeDtypeStruct((1 if dx else rows, 1 if dy else cols, S, V), jnp.float32) for dx, dy in ways
    ]
    return pl.pallas_call(
        functools.partial(halo_kernel, ways),
        in_specs=[pl.BlockSpec(memory_space=pl.ANY)],
        out_specs=[pl.BlockSpec(memory_space=pl.ANY)] * len(ways),
        out_shape=shapes,
        scratch_shapes=[pltpu.SemaphoreType.DMA((len(ways),)), pltpu.SemaphoreType.DMA((len(ways),))],
        compiler_params=pltpu.CompilerParams(collective_id=number, has_side_effects=True),
        name="halo" + str(number),
    )(grid)


def on_device(
    right_side,
    fine_coupling,
    fine_diagonal,
    fine_inverse,
    coarse_coupling,
    coarse_diagonal,
    coarse_inverse,
    coarse_pattern,
):
    index = window_index(
        coarse_pattern,
        HALF_X,
        BLOCK_Y,
        lax.axis_index("gx") * HALF_X,
        lax.axis_index("gy") * BLOCK_Y,
    ).reshape(-1)

    def fine(array):
        return array.reshape((BLOCK_X, BLOCK_Y) + array.shape[1:])

    def coarse(array):
        return array.reshape((HALF_X, BLOCK_Y) + array.shape[1:])

    fine_first = fine(first_sweep(right_side, fine_inverse))
    cells_last = fine_coupling.transpose(1, 2, 3, 0).reshape(S, 4 * S, -1)
    fine_matrix = fine(lax.optimization_barrier(cells_last).transpose(2, 0, 1))
    coarse_matrix = coarse(coarse_coupling.reshape(-1, S, 8 * S))
    b = fine(right_side)
    fine_iterate = fine_smooth(
        [fine_first] + edges(fine_first), fine_matrix, fine(fine_diagonal), fine(fine_inverse), b
    )
    side, coarse_first = fine_residue(
        [fine_iterate, *halo(fine_iterate, SIDES, 0)], fine_matrix, fine(fine_diagonal), b, coarse(coarse_inverse)
    )
    specs = [part_c(1, CW, S, 8 * S), part_c(1, CW, S, S)]
    coarse_iterate = coarse_call(
        coarse_smooth_kernel, "coarse_smooth", index,
        [coarse_first, *halo(coarse_first, SIDES + CORNERS, 1)],
        [coarse_matrix, coarse(coarse_diagonal), coarse(coarse_inverse), side],
        specs + [part_c(1, CW, S, S), part_c(1, CW, S, V)],
        BLOCK_Y,
    )
    next_side = coarse_call(
        coarse_residue_kernel, "coarse_residue", index,
        [coarse_iterate, *halo(coarse_iterate, SIDES + CORNERS, 2)],
        [coarse_matrix, coarse(coarse_diagonal), side],
        specs + [part_c(1, CW, S, V)],
        BLOCK_Y // 2,
    )
    return (
        fine_iterate.reshape(-1, S, V),
        coarse_iterate.reshape(-1, S, V),
        next_side.reshape(-1, S, V),
    )


def solution(mesh):
    cell = P(("gx", "gy"), None, None)
    placed = (
        cell,
        P(("gx", "gy"), None, None, None),
        cell,
        cell,
        P(("gx", "gy"), None, None, None),
        cell,
        cell,
        P(("gx", "gy"), None),
    )
    return jax.shard_map(
        on_device,
        mesh=mesh,
        in_specs=placed,
        out_specs=(cell, cell, cell),
        check_vma=False,
    )
```
